512 devices in a mesh: row: 32 (over x, z), col: 16 (over y, core).
Axes of the slice: x: 4, y: 8, z: 8, core: 2. Of those that a mesh axis runs over, the one named last changes fastest.
Arguments:
- window: float32 [16384, 16384], P('row', 'col'), may hold values from -6 to 6
- leaf_vecs: float32 [2, 16384, 128], P(None, ('row', 'col')), may hold values from -0.25 to 0.25
- leaf_t: float32 [2, 4096, 128], P(None, 'row'), may hold values from -0.25 to 0.25
- node_vecs: float32 [2, 4096, 128], P(None, 'row'), may hold values from -0.5 to 0.5
- node_t: float32 [2, 4096, 128], P(None, 'row'), may hold values from -0.25 to 0.25
Outputs:
- updated: float32 [16384, 16384], P('row', 'col')
The draws below stay inside these ranges and needn't reach their ends.
All inputs are finite; a program needn't handle non-finite values.
Results may differ from the reference program's by a relative error of at most 0.0002.
Values sent between devices are 32-bit elements; how exact they have to be, the bound alone decides.
A program may use at most 64 MiB of HBM per device.

```python
import jax
import jax.numpy as jnp
from jax import lax

NB = 128
NPAN = 2
NCOLS = 16384
MR_DEV = 512
M = 16384
N_ROW = 32


def block_scale(rng, extent, cuts, least, top_value):
    loudness = 1.0
    for position, parts in cuts:
        heights = jax.random.uniform(jax.random.fold_in(jax.random.fold_in(rng, 6), position), (parts,), jnp.float32, least / len(cuts), top_value / len(cuts))
        loudness = loudness * jnp.repeat(jnp.exp(heights), extent[position] // parts).reshape((-1,) + (1,) * (len(extent) - 1 - position))
    return loudness


def scatter_about(own_key, dims, width, bound, pieces=(), held_as=jnp.bfloat16):
    values = width * jax.random.normal(own_key, dims, jnp.float32)
    if pieces:
        values = values * block_scale(own_key, dims, pieces, -0.22, 0.18)
    return jnp.clip(values, -bound, bound).astype(held_as)


def setup_inputs(seed: int = 0) -> dict:
    arg_keys = jax.random.split(jax.random.key(seed), 6)
    return {
        "window": scatter_about(arg_keys[0], (M, NCOLS), 1.0, 6.0, ((0, 32), (1, 16)), jnp.float32),
        "leaf_vecs": scatter_about(arg_keys[1], (NPAN, M, NB), MR_DEV ** -0.5, 0.25, ((1, 512),), jnp.float32),
        "leaf_t": scatter_about(arg_keys[2], (NPAN, N_ROW * NB, NB), (4 * NB) ** -0.5, 0.25, ((1, 32),), jnp.float32),
        "node_vecs": scatter_about(arg_keys[3], (NPAN, N_ROW * NB, NB), NB ** -0.5, 0.5, ((1, 32),), jnp.float32),
        "node_t": scatter_about(arg_keys[4], (NPAN, N_ROW * NB, NB), (4 * NB) ** -0.5, 0.25, ((1, 32),), jnp.float32),
    }


def matmul(left, right):
    return jnp.dot(left, right, precision=lax.Precision.HIGHEST, preferred_element_type=jnp.float32)


def bmm(form, left, right):
    return jnp.einsum(form, left, right, precision=lax.Precision.HIGHEST)


def reference(window, leaf_vecs, leaf_t, node_vecs, node_t):
    levels = N_ROW.bit_length() - 1
    blocks = window.reshape(N_ROW, MR_DEV, NCOLS)
    for panel in range(NPAN):
        vecs = leaf_vecs[panel].reshape(N_ROW, MR_DEV, NB)
        lfac = leaf_t[panel].reshape(N_ROW, NB, NB)
        nvec = node_vecs[panel].reshape(N_ROW, NB, NB)
        nfac = node_t[panel].reshape(N_ROW, NB, NB)
        inner = bmm("rmk,rmn->rkn", vecs, blocks)
        inner = bmm("rjk,rjn->rkn", lfac, inner)
        blocks = blocks - bmm("rmk,rkn->rmn", vecs, inner)
        tops = blocks[:, :NB, :]
        for level in range(levels):
            stride = 1 << level
            lower_list = [index for index in range(N_ROW) if (index >> level) % 2 == 0]
            lower_ids = jnp.array(lower_list, dtype=jnp.int32)
            upper_ids = lower_ids + stride
            top_a = tops[lower_ids]
            top_b = tops[upper_ids]
            vb = nvec[upper_ids]
            sb = nfac[upper_ids]
            weight = top_a + bmm("rjk,rjn->rkn", vb, top_b)
            weight = bmm("rjk,rjn->rkn", sb, weight)
            tops = tops.at[lower_ids].set(top_a - weight)
            tops = tops.at[upper_ids].set(top_b - bmm("rkj,rjn->rkn", vb, weight))
        root = tops[0]
        inner = matmul(nvec[0].T, root)
        inner = matmul(nfac[0].T, inner)
        tops = tops.at[0].set(root - matmul(nvec[0], inner))
        blocks = jnp.concatenate([tops, blocks[:, NB:, :]], axis=1)
    return blocks.reshape(M, NCOLS)
```

```python
import functools

import jax
import jax.numpy as jnp
from jax import lax
from jax.experimental import pallas as pl
from jax.experimental.pallas import tpu as pltpu
from jax.sharding import PartitionSpec as P

MESH = pl.DeviceIdType.MESH
F32, BF16 = jnp.float32, jnp.bfloat16
NB = 128
NX = 4
CORES = 2
CHUNKS = 2


def split(value):
    high = value.astype(BF16)
    return high, (value - high.astype(F32)).astype(BF16)


def dot(left, right):
    return jnp.dot(left, right, preferred_element_type=F32)


def dot_nt(left, right):
    return lax.dot_general(left, right, (((1,), (1,)), ((), ())), preferred_element_type=F32)


def wide(value):
    high, low = split(value)
    return jnp.concatenate([high, high, low], axis=1)


def tall(value):
    high, low = split(value)
    return jnp.concatenate([high, high, low], axis=0)


def mixed(value, axis):
    high, low = split(value)
    return jnp.concatenate([high, low, high], axis=axis)


def kernel(sizes, *refs):
    nx, nz, ny, nc, mr, ncl, npan = sizes
    (window, leaf_vecs, leaf_t, node_vecs, node_t, out,
     work, yvec, lfac, vsz, vsx, stay, tz, tx, back, part, inn,
     yk, yt, lk, zv1, zs1, zvn, xv1, xs1, xvn,
     loc, barrier_free, ys, yr, ps, pr, hs, hr, zs, zr, xs, xr, ls, lr, osem) = refs
    del barrier_free
    cw = ncl // nc
    zc = cw // nz
    zx = zc // nx
    tw = min(256, cw)
    tiles = cw // tw
    me_r, me_c = lax.axis_index("row"), lax.axis_index("col")
    x, z = me_r // nz, lax.rem(me_r, nz)
    y, core = me_c // CORES, lax.rem(me_c, CORES)
    other = 1 - core

    def wait(sem, ref):
        pltpu.make_async_copy(ref, ref, sem).wait()

    def near(src, dst, sem):
        pltpu.make_async_copy(src, dst, sem).start()

    def far(src, dst, ssem, rsem, row, col):
        pltpu.make_async_remote_copy(
            src_ref=src, dst_ref=dst, send_sem=ssem, recv_sem=rsem,
            device_id={"row": row, "col": col}, device_id_type=MESH,
        ).start()

    def order(n):
        steps = []
        for d in range(n // 2, 0, -1):
            steps.append(d)
            if n - d != d:
                steps.append(n - d)
        return steps

    near(window, work, loc.at[0])
    for p in range(npan):
        near(leaf_vecs.at[p], yvec.at[p, y, core], loc.at[1])
        near(node_vecs.at[p, me_c], vsz.at[p, y, core, z, 0], loc.at[2])
        near(node_t.at[p, me_c], vsz.at[p, y, core, z, 1], loc.at[2])
        near(node_vecs.at[p, me_c], vsx.at[p, y, core, x, 0], loc.at[4])
        near(node_t.at[p, me_c], vsx.at[p, y, core, x, 1], loc.at[4])
    near(leaf_t, lfac, loc.at[3])

    barrier = pltpu.get_barrier_semaphore()
    for dx in range(nx):
        for dz in range(nz):
            if dx or dz:
                row = lax.rem(x + dx, nx) * nz + lax.rem(z + dz, nz)
                pl.semaphore_signal(barrier, inc=1, device_id={"row": row, "col": me_c}, device_id_type=MESH)
    for dy in range(1, ny):
        col = lax.rem(y + dy, ny) * CORES + core
        pl.semaphore_signal(barrier, inc=1, device_id={"row": me_r, "col": col}, device_id_type=MESH)
    pl.semaphore_signal(barrier, inc=1, device_id={"row": me_r, "col": y * CORES + other}, device_id_type=MESH)
    wait(loc.at[1], yvec.at[pl.ds(0, npan), 0, 0])
    wait(loc.at[2], vsz.at[pl.ds(0, npan), 0, 0, 0])
    wait(loc.at[4], vsx.at[pl.ds(0, npan), 0, 0, 0])
    pl.semaphore_wait(barrier, nx * nz - 1 + ny - 1 + 1)

    def send_y(p):
        for dy in order(ny):
            far(yvec.at[p, y, core], yvec.at[p, y, core], ys.at[p], yr.at[p], me_r, lax.rem(y + dy, ny) * CORES + core)

    def sibling(ref, ssem, rsem):
        far(ref, ref, ssem, rsem, me_r, y * CORES + other)

    def take_y(p):
        if ny > 1:
            wait(yr.at[p], yvec.at[p, pl.ds(0, ny - 1), 0])
        sibling(yvec.at[p, :, core], ps.at[0, p], pr.at[0, p])

    def send_first(p):
        for dz in order(nz):
            far(vsz.at[p, y, core, z], vsz.at[p, y, core, z], hs.at[0, 0, p], hr.at[0, 0, p],
                x * nz + lax.rem(z + dz, nz), me_c)
        for dx in order(nx):
            far(vsx.at[p, y, core, x], vsx.at[p, y, core, x], hs.at[0, 1, p], hr.at[0, 1, p],
                lax.rem(x + dx, nx) * nz + z, me_c)

    def send_second(k, p):
        buf, n = ((vsz, nz), (vsx, nx))[k]
        wait(hr.at[0, k, p], buf.at[p, 0, 0, pl.ds(0, n - 1)])
        for dy in order(ny):
            far(buf.at[p, y, core], buf.at[p, y, core], hs.at[1, k, p], hr.at[1, k, p],
                me_r, lax.rem(y + dy, ny) * CORES + core)

    def send_third(k, p):
        buf = (vsz, vsx)[k]
        if ny > 1:
            wait(hr.at[1, k, p], buf.at[p, pl.ds(0, ny - 1), 0])
        sibling(buf.at[p, :, core], ps.at[1 + k, p], pr.at[1 + k, p])

    send_y(0)
    for p in range(npan):
        if p:
            send_y(p)
        send_first(p)
    send_second(0, 0)
    take_y(0)
    send_second(1, 0)

    def prep_leaf(p):
        wait(pr.at[0, p], yvec.at[p, :, 0])
        vecs = yvec[p].reshape(mr, NB)
        yk[p] = mixed(vecs, 1)
        high, low = split(vecs.T)
        yt[p, :NB] = high
        yt[p, NB:] = low
        lk[p] = mixed(lfac[p].T, 1)

    wait(loc.at[3], lfac)
    prep_leaf(0)
    wait(loc.at[0], work)

    def reduce_rows(p, value, first, count):
        high, low = split(value)
        both = dot(yt[p, :, first:first + count], high)
        return both[:NB] + both[NB:] + dot(yt[p, :NB, first:first + count], low)

    def column(c, t):
        return pl.ds(pl.multiple_of(c * cw + t * tw, tw), tw)

    def leaf_top(p, c):
        @pl.loop(0, tiles)
        def _(t):
            cols = column(c, t)
            if p == 0:
                top = work[:NB, cols]
                inner = reduce_rows(p, work[:, cols], 0, mr)
            else:
                held = back.at[p - 1, c, pl.ds(t * (tw // zc), tw // zc)]
                top = held[...].reshape(tw, NB).T
                inner = part[:, cols] + reduce_rows(p, top, 0, NB)
            high, low = split(dot(lk[p], tall(inner)))
            stack = jnp.concatenate([high, high, low], axis=0)
            inn[:, cols] = stack
            top = top - dot(yk[p, :NB], stack)
            stay[p, c, pl.ds(t * (tw // zc), tw // zc)] = top.T.reshape(tw // zc, zc, NB)

    def send_z(p, c):
        near(stay.at[p, c, z], tz.at[p, c, z], zr.at[p, c])
        for dz in order(nz):
            zp = lax.rem(z + dz, nz)
            far(stay.at[p, c, zp], tz.at[p, c, z], zs.at[p, c], zr.at[p, c], x * nz + zp, me_c)

    def leaf_rest(p, c):
        @pl.loop(0, tiles)
        def _(t):
            cols = column(c, t)
            rest = work[NB:, cols] - dot(yk[p, NB:], inn[:, cols])
            work[NB:, cols] = rest

    def next_part(p, c):
        @pl.loop(0, tiles)
        def _(t):
            cols = column(c, t)
            part[:, cols] = reduce_rows(p, work[NB:, cols], NB, mr - NB)

    def prep_pairs(k, p):
        buf, n = ((vsz, nz), (vsx, nx))[k]
        v1, s1, vn = ((zv1, zs1, zvn), (xv1, xs1, xvn))[k]
        wait(pr.at[1 + k, p], buf.at[p, :, 0])

        @pl.loop(0, n)
        def _(b):
            vfac = buf[p, :, :, b, 0].reshape(NB, NB)
            high, low = split(vfac)
            v1[b] = jnp.concatenate([high, low, high], axis=0)
            vn[b] = jnp.concatenate([high, low, high], axis=1)
            s1[b] = mixed(buf[p, :, :, b, 1].reshape(NB, NB), 0)

    def pair(buf, rows, a, b, v1, s1, vn):
        top_a = buf[a].reshape(rows, NB)
        top_b = buf[b].reshape(rows, NB)
        weight = dot(wide(top_a + dot(wide(top_b), v1[b])), s1[b])
        return top_a - weight, top_b - dot_nt(wide(weight), vn[b])

    def level(buf, rows, n, bit, v1, s1, vn):
        shape = buf.shape[1:]
        for a in range(n):
            if a >> bit & 1 == 0:
                b = a | 1 << bit
                new_a, new_b = pair(buf, rows, a, b, v1, s1, vn)
                buf[a] = new_a.reshape(shape)
                buf[b] = new_b.reshape(shape)

    def z_stage(p, c):
        wait(zr.at[p, c], tz.at[p, c])
        for bit in range(nz.bit_length() - 1):
            level(tz.at[p, c], zc, nz, bit, zv1, zs1, zvn)

    def send_x(p, c):
        for dx in range(nx):
            xp = lax.rem(x + dx, nx)
            rows = pl.ds(pl.multiple_of(xp * zx, zx), zx)
            for dz in ([0] if dx == 0 else []) + order(nz) + ([0] if dx else []):
                zp = lax.rem(z + dz, nz)
                src, dst = tz.at[p, c, zp, rows], tx.at[p, c, x, z]
                if dx == 0 and dz == 0:
                    near(src, dst, xr.at[p, c])
                else:
                    far(src, dst, xs.at[p, c], xr.at[p, c], xp * nz + zp, me_c)

    def x_stage(p, c):
        wait(xr.at[p, c], tx.at[p, c])
        rows = nz * zx
        for bit in range(nx.bit_length() - 1):
            level(tx.at[p, c], rows, nx, bit, xv1, xs1, xvn)

        @pl.when(z == 0)
        def _():
            root = tx[p, c, 0].reshape(rows, NB)
            inner = dot(wide(dot(wide(root), xv1[0])), xs1[0])
            tx[p, c, 0] = (root - dot_nt(wide(inner), xvn[0])).reshape(nz, zx, NB)

    def send_l(p, c):
        near(tx.at[p, c, x], back.at[p, c, :, x], lr.at[p, c])
        for dx in order(nx):
            xp = lax.rem(x + dx, nx)
            far(tx.at[p, c, xp], back.at[p, c, :, x], ls.at[p, c], lr.at[p, c], xp * nz + z, me_c)

    def out_rest(c):
        cols = pl.ds(pl.multiple_of(c * cw, cw), cw)
        near(work.at[pl.ds(NB, mr - NB), cols], out.at[pl.ds(NB, mr - NB), cols], osem)

    for p in range(npan):
        @pl.loop(0, nc)
        def _(c):
            if p:
                wait(lr.at[p - 1, c], back.at[p - 1, c])
            leaf_top(p, c)
            send_z(p, c)

        if p == 0:
            send_third(0, 0)
            send_third(1, 0)
            for q in range(1, npan):
                take_y(q)
                send_second(0, q)
                send_second(1, q)
        prep_pairs(0, p)

        @pl.loop(0, nc)
        def _(c):
            leaf_rest(p, c)
            if p == npan - 1:
                out_rest(c)

        @pl.loop(0, nc)
        def _(c):
            z_stage(p, c)
            send_x(p, c)

        prep_pairs(1, p)
        if p + 1 < npan:
            prep_leaf(p + 1)
            send_third(0, p + 1)
            send_third(1, p + 1)

            @pl.loop(0, nc)
            def _(c):
                next_part(p + 1, c)

        @pl.loop(0, nc)
        def _(c):
            x_stage(p, c)
            send_l(p, c)

    last = npan - 1

    @pl.loop(0, nc)
    def _(c):
        wait(lr.at[last, c], back.at[last, c])

        @pl.loop(0, tiles)
        def _(t):
            cols = column(c, t)
            held = back.at[last, c, pl.ds(t * (tw // zc), tw // zc)]
            work[:NB, cols] = held[...].reshape(tw, NB).T
        cols = pl.ds(pl.multiple_of(c * cw, cw), cw)
        near(work.at[pl.ds(0, NB), cols], out.at[pl.ds(0, NB), cols], osem)

    wait(osem, work)
    for p in range(npan):
        if ny > 1:
            wait(ys.at[p], yvec.at[p, pl.ds(0, ny - 1), 0])
            for k, buf in ((0, vsz), (1, vsx)):
                wait(hs.at[1, k, p], buf.at[p, pl.ds(0, ny - 1), 0])
        wait(ps.at[0, p], yvec.at[p, :, 0])
        for k, (buf, n) in enumerate(((vsz, nz), (vsx, nx))):
            wait(hs.at[0, k, p], buf.at[p, 0, 0, pl.ds(0, n - 1)])
            wait(ps.at[1 + k, p], buf.at[p, :, 0])

        @pl.loop(0, nc)
        def _(c):
            wait(zs.at[p, c], stay.at[p, c, pl.ds(0, nz - 1)])
            wait(xs.at[p, c], tx.at[p, c, pl.ds(0, nx - 1)])
            wait(xs.at[p, c], tx.at[p, c, 0, pl.ds(0, nz - 1)])
            wait(ls.at[p, c], tx.at[p, c, pl.ds(0, nx - 1)])


def local(nx, nc, window, leaf_vecs, leaf_t, node_vecs, node_t):
    mr, ncl = window.shape
    npan = leaf_t.shape[0]
    nz = lax.axis_size("row") // nx
    nq = lax.axis_size("col")
    ny = nq // CORES
    vr = NB // nq
    cw = ncl // nc
    zc = cw // nz
    zx = zc // nx
    any_space = pl.BlockSpec(memory_space=pl.ANY)
    dma = pltpu.SemaphoreType.DMA
    scratch = [
        pltpu.VMEM((mr, ncl), F32),
        pltpu.VMEM((npan, ny, CORES, mr // nq, NB), F32),
        pltpu.VMEM((npan, NB, NB), F32),
        pltpu.VMEM((npan, ny, CORES, nz, 2, vr, NB), F32),
        pltpu.VMEM((npan, ny, CORES, nx, 2, vr, NB), F32),
        pltpu.VMEM((npan, nc, nz, zc, NB), F32),
        pltpu.VMEM((npan, nc, nz, zc, NB), F32),
        pltpu.VMEM((npan, nc, nx, nz, zx, NB), F32),
        pltpu.VMEM((npan, nc, nz, nx, zx, NB), F32),
        pltpu.VMEM((NB, ncl), F32),
        pltpu.VMEM((3 * NB, ncl), BF16),
        pltpu.VMEM((npan, mr, 3 * NB), BF16),
        pltpu.VMEM((npan, 2 * NB, mr), BF16),
        pltpu.VMEM((npan, NB, 3 * NB), BF16),
    ]
    for n in (nz, nx):
        scratch += [
            pltpu.VMEM((n, 3 * NB, NB), BF16),
            pltpu.VMEM((n, 3 * NB, NB), BF16),
            pltpu.VMEM((n, NB, 3 * NB), BF16),
        ]
    scratch += [
        dma((5,)), dma((1,)), dma((npan,)), dma((npan,)), dma((3, npan)), dma((3, npan)),
        dma((2, 2, npan)), dma((2, 2, npan)),
        dma((npan, nc)), dma((npan, nc)), dma((npan, nc)), dma((npan, nc)), dma((npan, nc)), dma((npan, nc)),
        dma,
    ]
    return pl.pallas_call(
        functools.partial(kernel, (nx, nz, ny, nc, mr, ncl, npan)),
        out_shape=jax.ShapeDtypeStruct(window.shape, window.dtype),
        in_specs=[any_space] * 5,
        out_specs=any_space,
        scratch_shapes=scratch,
        compiler_params=pltpu.CompilerParams(
            collective_id=0, has_side_effects=True, vmem_limit_bytes=48 * 1024 * 1024
        ),
    )(
        window, leaf_vecs, leaf_t,
        node_vecs.reshape(npan, nq, vr, NB), node_t.reshape(npan, nq, vr, NB),
    )


def build(mesh, nx, nc):
    placed = (
        P("row", "col"),
        P(None, ("row", "col"), None),
        P(None, "row", None),
        P(None, "row", None),
        P(None, "row", None),
    )
    return jax.shard_map(
        functools.partial(local, nx, nc), mesh=mesh, in_specs=placed, out_specs=P("row", "col"), check_vma=False
    )


def solution(mesh):
    return build(mesh, NX, CHUNKS)
```

```python
import functools

import jax
import jax.numpy as jnp
from jax import lax
from jax.experimental import pallas as pl
from jax.experimental.pallas import tpu as pltpu
from jax.sharding import PartitionSpec as P

MESH = pl.DeviceIdType.MESH
F32, BF16 = jnp.float32, jnp.bfloat16
NB = 128
NX = 4
CORES = 2
CHUNKS = 4


def split(value):
    high = value.astype(BF16)
    return high, (value - high.astype(F32)).astype(BF16)


def dot(left, right):
    return jnp.dot(left, right, preferred_element_type=F32)


def dot_nt(left, right):
    return lax.dot_general(left, right, (((1,), (1,)), ((), ())), preferred_element_type=F32)


def wide(value):
    high, low = split(value)
    return jnp.concatenate([high, high, low], axis=1)


def tall(value):
    high, low = split(value)
    return jnp.concatenate([high, high, low], axis=0)


def mixed(value, axis):
    high, low = split(value)
    return jnp.concatenate([high, low, high], axis=axis)


def kernel(sizes, *refs):
    nx, nz, ny, nc, mr, ncl, npan = sizes
    (window, leaf_vecs, leaf_t, node_vecs, node_t, out,
     work, yvec, lfac, vsz, vsx, stay, tz, tx, back, part, inn,
     yk, yt, lk, zv1, zs1, zvn, xv1, xs1, xvn,
     loc, barrier_free, ys, yr, ps, pr, hs, hr, zs, zr, xs, xr, ls, lr, osem) = refs
    del barrier_free
    cw = ncl // nc
    zc = cw // nz
    zx = zc // nx
    tw = min(256, cw)
    tiles = cw // tw
    me_r, me_c = lax.axis_index("row"), lax.axis_index("col")
    x, z = me_r // nz, lax.rem(me_r, nz)
    y, core = me_c // CORES, lax.rem(me_c, CORES)
    other = 1 - core

    def wait(sem, ref):
        pltpu.make_async_copy(ref, ref, sem).wait()

    def near(src, dst, sem):
        pltpu.make_async_copy(src, dst, sem).start()

    def far(src, dst, ssem, rsem, row, col):
        pltpu.make_async_remote_copy(
            src_ref=src, dst_ref=dst, send_sem=ssem, recv_sem=rsem,
            device_id={"row": row, "col": col}, device_id_type=MESH,
        ).start()

    def order(n):
        steps = []
        for d in range(n // 2, 0, -1):
            steps.append(d)
            if n - d != d:
                steps.append(n - d)
        return steps

    near(window, work, loc.at[0])
    for p in range(npan):
        near(leaf_vecs.at[p], yvec.at[p, y, core], loc.at[1])
        near(node_vecs.at[p, me_c], vsz.at[p, y, core, z, 0], loc.at[2])
        near(node_t.at[p, me_c], vsz.at[p, y, core, z, 1], loc.at[2])
        near(node_vecs.at[p, me_c], vsx.at[p, y, core, x, 0], loc.at[4])
        near(node_t.at[p, me_c], vsx.at[p, y, core, x, 1], loc.at[4])
    near(leaf_t, lfac, loc.at[3])

    barrier = pltpu.get_barrier_semaphore()
    for dx in range(nx):
        for dz in range(nz):
            if dx or dz:
                row = lax.rem(x + dx, nx) * nz + lax.rem(z + dz, nz)
                pl.semaphore_signal(barrier, inc=1, device_id={"row": row, "col": me_c}, device_id_type=MESH)
    for dy in range(1, ny):
        col = lax.rem(y + dy, ny) * CORES + core
        pl.semaphore_signal(barrier, inc=1, device_id={"row": me_r, "col": col}, device_id_type=MESH)
    pl.semaphore_signal(barrier, inc=1, device_id={"row": me_r, "col": y * CORES + other}, device_id_type=MESH)
    wait(loc.at[1], yvec.at[pl.ds(0, npan), 0, 0])
    wait(loc.at[2], vsz.at[pl.ds(0, npan), 0, 0, 0])
    wait(loc.at[4], vsx.at[pl.ds(0, npan), 0, 0, 0])
    pl.semaphore_wait(barrier, nx * nz - 1 + ny - 1 + 1)

    turn = 1 - 2 * core
    rings = (yvec, vsz, vsx)

    def place(shift):
        return lax.rem(y + turn * shift + 2 * ny, ny)

    ahead, behind = ny // 2, (ny - 1) // 2

    def ring_wait(kind, p, step):
        if step < ahead:
            wait(yr.at[kind, p, step], rings[kind].at[p, 0, core])
        if step < behind:
            wait(yr.at[kind, p, ahead + step], rings[kind].at[p, 0, core])

    def ring_step(kind, p, step):
        if step:
            ring_wait(kind, p, step - 1)
        if step < ahead:
            piece = rings[kind].at[p, place(-step), core]
            far(piece, piece, ys.at[kind, p, step], yr.at[kind, p, step], me_r, place(1) * CORES + core)
        if step < behind:
            piece = rings[kind].at[p, place(step), core]
            far(piece, piece, ys.at[kind, p, ahead + step], yr.at[kind, p, ahead + step],
                me_r, place(-1) * CORES + core)

    def ring_end(kind, p):
        ring_wait(kind, p, ahead - 1)
        ref = rings[kind].at[p, :, core]
        far(ref, ref, ps.at[kind, p], pr.at[kind, p], me_r, y * CORES + other)

    def first_wait(k, p):
        buf, n = ((vsz, nz), (vsx, nx))[k]
        wait(hr.at[0, k, p], buf.at[p, 0, 0, pl.ds(0, n - 1)])

    def send_first(p):
        for dz in order(nz):
            far(vsz.at[p, y, core, z], vsz.at[p, y, core, z], hs.at[0, 0, p], hr.at[0, 0, p],
                x * nz + lax.rem(z + dz, nz), me_c)
        for dx in order(nx):
            far(vsx.at[p, y, core, x], vsx.at[p, y, core, x], hs.at[0, 1, p], hr.at[0, 1, p],
                lax.rem(x + dx, nx) * nz + z, me_c)

    for p in range(npan):
        send_first(p)
    ring_step(0, 0, 0)
    ring_step(0, 0, 1)
    first_wait(0, 0)
    ring_step(1, 0, 0)
    ring_step(0, 0, 2)
    ring_step(1, 0, 1)
    ring_step(0, 0, 3)
    first_wait(1, 0)
    ring_end(0, 0)
    ring_step(1, 0, 2)
    ring_step(2, 0, 0)

    def prep_leaf(p):
        wait(pr.at[0, p], yvec.at[p, :, 0])
        vecs = yvec[p].reshape(mr, NB)
        yk[p] = mixed(vecs, 1)
        high, low = split(vecs.T)
        yt[p, :NB] = high
        yt[p, NB:] = low
        lk[p] = mixed(lfac[p].T, 1)

    wait(loc.at[3], lfac)
    prep_leaf(0)
    wait(loc.at[0], work)

    def reduce_rows(p, value, first, count):
        high, low = split(value)
        both = dot(yt[p, :, first:first + count], high)
        return both[:NB] + both[NB:] + dot(yt[p, :NB, first:first + count], low)

    def column(c, t):
        return pl.ds(pl.multiple_of(c * cw + t * tw, tw), tw)

    def leaf_top(p, c):
        @pl.loop(0, tiles)
        def _(t):
            cols = column(c, t)
            if p == 0:
                top = work[:NB, cols]
                inner = reduce_rows(p, work[:, cols], 0, mr)
            else:
                held = back.at[p - 1, c, pl.ds(t * (tw // zc), tw // zc)]
                top = held[...].reshape(tw, NB).T
                inner = part[:, cols] + reduce_rows(p, top, 0, NB)
            high, low = split(dot(lk[p], tall(inner)))
            stack = jnp.concatenate([high, high, low], axis=0)
            inn[:, cols] = stack
            top = top - dot(yk[p, :NB], stack)
            stay[p, c, pl.ds(t * (tw // zc), tw // zc)] = top.T.reshape(tw // zc, zc, NB)

    def send_z(p, c):
        near(stay.at[p, c, z], tz.at[p, c, z], zr.at[p, c])
        for dz in order(nz):
            zp = lax.rem(z + dz, nz)
            far(stay.at[p, c, zp], tz.at[p, c, z], zs.at[p, c], zr.at[p, c], x * nz + zp, me_c)

    def leaf_rest(p, c):
        @pl.loop(0, tiles)
        def _(t):
            cols = column(c, t)
            rest = work[NB:, cols] - dot(yk[p, NB:], inn[:, cols])
            work[NB:, cols] = rest

    def next_part(p, c):
        @pl.loop(0, tiles)
        def _(t):
            cols = column(c, t)
            part[:, cols] = reduce_rows(p, work[NB:, cols], NB, mr - NB)

    def prep_pairs(k, p):
        buf, n = ((vsz, nz), (vsx, nx))[k]
        v1, s1, vn = ((zv1, zs1, zvn), (xv1, xs1, xvn))[k]
        wait(pr.at[1 + k, p], buf.at[p, :, 0])

        @pl.loop(0, n)
        def _(b):
            vfac = buf[p, :, :, b, 0].reshape(NB, NB)
            high, low = split(vfac)
            v1[b] = jnp.concatenate([high, low, high], axis=0)
            vn[b] = jnp.concatenate([high, low, high], axis=1)
            s1[b] = mixed(buf[p, :, :, b, 1].reshape(NB, NB), 0)

    def pair(buf, rows, a, b, v1, s1, vn):
        top_a = buf[a].reshape(rows, NB)
        top_b = buf[b].reshape(rows, NB)
        weight = dot(wide(top_a + dot(wide(top_b), v1[b])), s1[b])
        return top_a - weight, top_b - dot_nt(wide(weight), vn[b])

    def level(buf, rows, n, bit, v1, s1, vn):
        shape = buf.shape[1:]
        for a in range(n):
            if a >> bit & 1 == 0:
                b = a | 1 << bit
                new_a, new_b = pair(buf, rows, a, b, v1, s1, vn)
                buf[a] = new_a.reshape(shape)
                buf[b] = new_b.reshape(shape)

    def z_stage(p, c):
        wait(zr.at[p, c], tz.at[p, c])
        for bit in range(nz.bit_length() - 1):
            level(tz.at[p, c], zc, nz, bit, zv1, zs1, zvn)

    def send_x(p, c):
        for dx in range(nx):
            xp = lax.rem(x + dx, nx)
            rows = pl.ds(pl.multiple_of(xp * zx, zx), zx)
            for dz in ([0] if dx == 0 else []) + order(nz) + ([0] if dx else []):
                zp = lax.rem(z + dz, nz)
                src, dst = tz.at[p, c, zp, rows], tx.at[p, c, x, z]
                if dx == 0 and dz == 0:
                    near(src, dst, xr.at[p, c])
                else:
                    far(src, dst, xs.at[p, c], xr.at[p, c], xp * nz + zp, me_c)

    def x_stage(p, c):
        wait(xr.at[p, c], tx.at[p, c])
        rows = nz * zx
        for bit in range(nx.bit_length() - 1):
            level(tx.at[p, c], rows, nx, bit, xv1, xs1, xvn)

        @pl.when(z == 0)
        def _():
            root = tx[p, c, 0].reshape(rows, NB)
            inner = dot(wide(dot(wide(root), xv1[0])), xs1[0])
            tx[p, c, 0] = (root - dot_nt(wide(inner), xvn[0])).reshape(nz, zx, NB)

    def send_l(p, c):
        near(tx.at[p, c, x], back.at[p, c, :, x], lr.at[p, c])
        for dx in order(nx):
            xp = lax.rem(x + dx, nx)
            far(tx.at[p, c, xp], back.at[p, c, :, x], ls.at[p, c], lr.at[p, c], xp * nz + z, me_c)

    def out_rest(c):
        cols = pl.ds(pl.multiple_of(c * cw, cw), cw)
        near(work.at[pl.ds(NB, mr - NB), cols], out.at[pl.ds(NB, mr - NB), cols], osem)

    for p in range(npan):
        @pl.loop(0, nc)
        def _(c):
            if p:
                wait(lr.at[p - 1, c], back.at[p - 1, c])
            leaf_top(p, c)
            send_z(p, c)

        if p == 0:
            ring_step(1, 0, 3)
            ring_step(2, 0, 1)
        else:
            ring_end(2, p)

        @pl.loop(0, nc)
        def _(c):
            leaf_rest(p, c)
            if p == npan - 1:
                out_rest(c)

        if p == 0:
            ring_end(1, 0)
            ring_step(2, 0, 2)
            ring_step(2, 0, 3)
            for q in range(1, npan):
                first_wait(0, q)
                first_wait(1, q)
        prep_pairs(0, p)
        if p == 0:
            ring_end(2, 0)

        @pl.loop(0, nc)
        def _(c):
            z_stage(p, c)
            send_x(p, c)
            if p + 1 < npan:
                for step in range(ahead):
                    @pl.when(c == step)
                    def _():
                        ring_step(0, p + 1, step)
                        ring_step(1, p + 1, step)

        if p + 1 < npan:
            ring_end(0, p + 1)
            ring_end(1, p + 1)
        prep_pairs(1, p)
        if p + 1 < npan:
            prep_leaf(p + 1)

            @pl.loop(0, nc)
            def _(c):
                next_part(p + 1, c)

        @pl.loop(0, nc)
        def _(c):
            x_stage(p, c)
            send_l(p, c)
            if p + 1 < npan:
                for step in range(ahead):
                    @pl.when(c == step)
                    def _():
                        ring_step(2, p + 1, step)

    last = npan - 1

    @pl.loop(0, nc)
    def _(c):
        wait(lr.at[last, c], back.at[last, c])

        @pl.loop(0, tiles)
        def _(t):
            cols = column(c, t)
            held = back.at[last, c, pl.ds(t * (tw // zc), tw // zc)]
            work[:NB, cols] = held[...].reshape(tw, NB).T
        cols = pl.ds(pl.multiple_of(c * cw, cw), cw)
        near(work.at[pl.ds(0, NB), cols], out.at[pl.ds(0, NB), cols], osem)

    wait(osem, work)
    for p in range(npan):
        for kind in range(3):
            for step in range(ny - 1):
                wait(ys.at[kind, p, step], rings[kind].at[p, 0, core])
        wait(ps.at[0, p], yvec.at[p, :, 0])
        for k, (buf, n) in enumerate(((vsz, nz), (vsx, nx))):
            wait(hs.at[0, k, p], buf.at[p, 0, 0, pl.ds(0, n - 1)])
            wait(ps.at[1 + k, p], buf.at[p, :, 0])

        @pl.loop(0, nc)
        def _(c):
            wait(zs.at[p, c], stay.at[p, c, pl.ds(0, nz - 1)])
            wait(xs.at[p, c], tx.at[p, c, pl.ds(0, nx - 1)])
            wait(xs.at[p, c], tx.at[p, c, 0, pl.ds(0, nz - 1)])
            wait(ls.at[p, c], tx.at[p, c, pl.ds(0, nx - 1)])


def local(nx, nc, window, leaf_vecs, leaf_t, node_vecs, node_t):
    mr, ncl = window.shape
    npan = leaf_t.shape[0]
    nz = lax.axis_size("row") // nx
    nq = lax.axis_size("col")
    ny = nq // CORES
    vr = NB // nq
    cw = ncl // nc
    zc = cw // nz
    zx = zc // nx
    any_space = pl.BlockSpec(memory_space=pl.ANY)
    dma = pltpu.SemaphoreType.DMA
    scratch = [
        pltpu.VMEM((mr, ncl), F32),
        pltpu.VMEM((npan, ny, CORES, mr // nq, NB), F32),
        pltpu.VMEM((npan, NB, NB), F32),
        pltpu.VMEM((npan, ny, CORES, nz, 2, vr, NB), F32),
        pltpu.VMEM((npan, ny, CORES, nx, 2, vr, NB), F32),
        pltpu.VMEM((npan, nc, nz, zc, NB), F32),
        pltpu.VMEM((npan, nc, nz, zc, NB), F32),
        pltpu.VMEM((npan, nc, nx, nz, zx, NB), F32),
        pltpu.VMEM((npan, nc, nz, nx, zx, NB), F32),
        pltpu.VMEM((NB, ncl), F32),
        pltpu.VMEM((3 * NB, ncl), BF16),
        pltpu.VMEM((npan, mr, 3 * NB), BF16),
        pltpu.VMEM((npan, 2 * NB, mr), BF16),
        pltpu.VMEM((npan, NB, 3 * NB), BF16),
    ]
    for n in (nz, nx):
        scratch += [
            pltpu.VMEM((n, 3 * NB, NB), BF16),
            pltpu.VMEM((n, 3 * NB, NB), BF16),
            pltpu.VMEM((n, NB, 3 * NB), BF16),
        ]
    scratch += [
        dma((5,)), dma((1,)), dma((3, npan, ny - 1)), dma((3, npan, ny - 1)), dma((3, npan)), dma((3, npan)),
        dma((1, 2, npan)), dma((1, 2, npan)),
        dma((npan, nc)), dma((npan, nc)), dma((npan, nc)), dma((npan, nc)), dma((npan, nc)), dma((npan, nc)),
        dma,
    ]
    return pl.pallas_call(
        functools.partial(kernel, (nx, nz, ny, nc, mr, ncl, npan)),
        out_shape=jax.ShapeDtypeStruct(window.shape, window.dtype),
        in_specs=[any_space] * 5,
        out_specs=any_space,
        scratch_shapes=scratch,
        compiler_params=pltpu.CompilerParams(
            collective_id=0, has_side_effects=True, vmem_limit_bytes=67_043_328
        ),
    )(
        window, leaf_vecs, leaf_t,
        node_vecs.reshape(npan, nq, vr, NB), node_t.reshape(npan, nq, vr, NB),
    )


def build(mesh, nx, nc):
    placed = (
        P("row", "col"),
        P(None, ("row", "col"), None),
        P(None, "row", None),
        P(None, "row", None),
        P(None, "row", None),
    )
    return jax.shard_map(
        functools.partial(local, nx, nc), mesh=mesh, in_specs=placed, out_specs=P("row", "col"), check_vma=False
    )


def solution(mesh):
    return build(mesh, NX, CHUNKS)
```

```python
import functools

import jax
import jax.numpy as jnp
from jax import lax
from jax.experimental import pallas as pl
from jax.experimental.pallas import tpu as pltpu
from jax.sharding import PartitionSpec as P

MESH = pl.DeviceIdType.MESH
F32, BF16 = jnp.float32, jnp.bfloat16
NB = 128
NX = 4
CORES = 2
CHUNKS = 4


def split(value):
    high = value.astype(BF16)
    return high, (value - high.astype(F32)).astype(BF16)


def dot(left, right):
    return jnp.dot(left, right, preferred_element_type=F32)


def dot_nt(left, right):
    return lax.dot_general(left, right, (((1,), (1,)), ((), ())), preferred_element_type=F32)


def wide(value):
    high, low = split(value)
    return jnp.concatenate([high, high, low], axis=1)


def tall(value):
    high, low = split(value)
    return jnp.concatenate([high, high, low], axis=0)


def mixed(value, axis):
    high, low = split(value)
    return jnp.concatenate([high, low, high], axis=axis)


def kernel(sizes, *refs):
    nx, nz, ny, nc, mr, ncl, npan = sizes
    (window, leaf_vecs, leaf_t, node_vecs, node_t, out,
     work, yvec, lfac, vsz, vsx, stay, tz, tx, back, part, inn,
     yk, yt, lk, zv1, zs1, zvn, xv1, xs1, xvn,
     loc, barrier_free, ys, yr, ps, pr, hs, hr, zs, zr, xs, xr, ls, lr, osem) = refs
    del barrier_free
    cw = ncl // nc
    zc = cw // nz
    zx = zc // nx
    tw = min(256, cw)
    tiles = cw // tw
    me_r, me_c = lax.axis_index("row"), lax.axis_index("col")
    x, z = me_r // nz, lax.rem(me_r, nz)
    y, core = me_c // CORES, lax.rem(me_c, CORES)
    other = 1 - core

    def wait(sem, ref):
        pltpu.make_async_copy(ref, ref, sem).wait()

    def near(src, dst, sem):
        pltpu.make_async_copy(src, dst, sem).start()

    def far(src, dst, ssem, rsem, row, col):
        pltpu.make_async_remote_copy(
            src_ref=src, dst_ref=dst, send_sem=ssem, recv_sem=rsem,
            device_id={"row": row, "col": col}, device_id_type=MESH,
        ).start()

    def order(n):
        steps = []
        for d in range(n // 2, 0, -1):
            steps.append(d)
            if n - d != d:
                steps.append(n - d)
        return steps

    near(window, work, loc.at[0])
    for p in range(npan):
        near(leaf_vecs.at[p], yvec.at[p, y, core], loc.at[1])
        near(node_vecs.at[p, me_c], vsz.at[p, y, core, z, 0], loc.at[2])
        near(node_t.at[p, me_c], vsz.at[p, y, core, z, 1], loc.at[2])
        near(node_vecs.at[p, me_c], vsx.at[p, y, core, x, 0], loc.at[4])
        near(node_t.at[p, me_c], vsx.at[p, y, core, x, 1], loc.at[4])
    near(leaf_t, lfac, loc.at[3])

    barrier = pltpu.get_barrier_semaphore()
    for dx in range(nx):
        for dz in range(nz):
            if dx or dz:
                row = lax.rem(x + dx, nx) * nz + lax.rem(z + dz, nz)
                pl.semaphore_signal(barrier, inc=1, device_id={"row": row, "col": me_c}, device_id_type=MESH)
    for dy in range(1, ny):
        col = lax.rem(y + dy, ny) * CORES + core
        pl.semaphore_signal(barrier, inc=1, device_id={"row": me_r, "col": col}, device_id_type=MESH)
    pl.semaphore_signal(barrier, inc=1, device_id={"row": me_r, "col": y * CORES + other}, device_id_type=MESH)
    wait(loc.at[1], yvec.at[pl.ds(0, npan), 0, 0])
    wait(loc.at[2], vsz.at[pl.ds(0, npan), 0, 0, 0])
    wait(loc.at[4], vsx.at[pl.ds(0, npan), 0, 0, 0])
    pl.semaphore_wait(barrier, nx * nz - 1 + ny - 1 + 1)

    def send_y(p):
        for dy in order(ny):
            far(yvec.at[p, y, core], yvec.at[p, y, core], ys.at[p], yr.at[p], me_r, lax.rem(y + dy, ny) * CORES + core)

    def sibling(ref, ssem, rsem):
        far(ref, ref, ssem, rsem, me_r, y * CORES + other)

    def take_y(p):
        if ny > 1:
            wait(yr.at[p], yvec.at[p, pl.ds(0, ny - 1), 0])
        sibling(yvec.at[p, :, core], ps.at[0, p], pr.at[0, p])

    def send_first(p):
        for dz in order(nz):
            far(vsz.at[p, y, core, z], vsz.at[p, y, core, z], hs.at[0, 0, p], hr.at[0, 0, p],
                x * nz + lax.rem(z + dz, nz), me_c)
        for dx in order(nx):
            far(vsx.at[p, y, core, x], vsx.at[p, y, core, x], hs.at[0, 1, p], hr.at[0, 1, p],
                lax.rem(x + dx, nx) * nz + z, me_c)

    def send_second(k, p):
        buf, n = ((vsz, nz), (vsx, nx))[k]
        wait(hr.at[0, k, p], buf.at[p, 0, 0, pl.ds(0, n - 1)])
        for dy in order(ny):
            far(buf.at[p, y, core], buf.at[p, y, core], hs.at[1, k, p], hr.at[1, k, p],
                me_r, lax.rem(y + dy, ny) * CORES + core)

    def send_third(k, p):
        buf = (vsz, vsx)[k]
        if ny > 1:
            wait(hr.at[1, k, p], buf.at[p, pl.ds(0, ny - 1), 0])
        sibling(buf.at[p, :, core], ps.at[1 + k, p], pr.at[1 + k, p])

    send_y(0)
    for p in range(npan):
        if p:
            send_y(p)
        send_first(p)
    send_second(0, 0)
    take_y(0)
    send_second(1, 0)

    def prep_leaf(p):
        wait(pr.at[0, p], yvec.at[p, :, 0])
        vecs = yvec[p].reshape(mr, NB)
        yk[p] = mixed(vecs, 1)
        high, low = split(vecs.T)
        yt[p, :NB] = high
        yt[p, NB:] = low
        lk[p] = mixed(lfac[p].T, 1)

    wait(loc.at[3], lfac)
    prep_leaf(0)
    wait(loc.at[0], work)

    def reduce_rows(p, value, first, count):
        high, low = split(value)
        both = dot(yt[p, :, first:first + count], high)
        return both[:NB] + both[NB:] + dot(yt[p, :NB, first:first + count], low)

    def column(c, t):
        return pl.ds(pl.multiple_of(c * cw + t * tw, tw), tw)

    def leaf_top(p, c):
        @pl.loop(0, tiles)
        def _(t):
            cols = column(c, t)
            if p == 0:
                top = work[:NB, cols]
                inner = reduce_rows(p, work[:, cols], 0, mr)
            else:
                held = back.at[p - 1, c, pl.ds(t * (tw // zc), tw // zc)]
                top = held[...].reshape(tw, NB).T
                inner = part[:, cols] + reduce_rows(p, top, 0, NB)
            high, low = split(dot(lk[p], tall(inner)))
            stack = jnp.concatenate([high, high, low], axis=0)
            inn[:, cols] = stack
            top = top - dot(yk[p, :NB], stack)
            stay[p, c, pl.ds(t * (tw // zc), tw // zc)] = top.T.reshape(tw // zc, zc, NB)

    def send_z(p, c):
        near(stay.at[p, c, z], tz.at[p, c, z], zr.at[p, c])
        for dz in order(nz):
            zp = lax.rem(z + dz, nz)
            far(stay.at[p, c, zp], tz.at[p, c, z], zs.at[p, c], zr.at[p, c], x * nz + zp, me_c)

    def leaf_rest(p, c):
        @pl.loop(0, tiles)
        def _(t):
            cols = column(c, t)
            rest = work[NB:, cols] - dot(yk[p, NB:], inn[:, cols])
            work[NB:, cols] = rest

    def next_part(p, c):
        @pl.loop(0, tiles)
        def _(t):
            cols = column(c, t)
            part[:, cols] = reduce_rows(p, work[NB:, cols], NB, mr - NB)

    def prep_pairs(k, p):
        buf, n = ((vsz, nz), (vsx, nx))[k]
        v1, s1, vn = ((zv1, zs1, zvn), (xv1, xs1, xvn))[k]
        wait(pr.at[1 + k, p], buf.at[p, :, 0])

        @pl.loop(0, n)
        def _(b):
            vfac = buf[p, :, :, b, 0].reshape(NB, NB)
            high, low = split(vfac)
            v1[b] = jnp.concatenate([high, low, high], axis=0)
            vn[b] = jnp.concatenate([high, low, high], axis=1)
            s1[b] = mixed(buf[p, :, :, b, 1].reshape(NB, NB), 0)

    def pair(buf, rows, a, b, v1, s1, vn):
        top_a = buf[a].reshape(rows, NB)
        top_b = buf[b].reshape(rows, NB)
        weight = dot(wide(top_a + dot(wide(top_b), v1[b])), s1[b])
        return top_a - weight, top_b - dot_nt(wide(weight), vn[b])

    def level(buf, rows, n, bit, v1, s1, vn):
        shape = buf.shape[1:]
        for a in range(n):
            if a >> bit & 1 == 0:
                b = a | 1 << bit
                new_a, new_b = pair(buf, rows, a, b, v1, s1, vn)
                buf[a] = new_a.reshape(shape)
                buf[b] = new_b.reshape(shape)

    def z_stage(p, c):
        wait(zr.at[p, c], tz.at[p, c])
        for bit in range(nz.bit_length() - 1):
            level(tz.at[p, c], zc, nz, bit, zv1, zs1, zvn)

    def send_x(p, c):
        for dx in range(nx):
            xp = lax.rem(x + dx, nx)
            rows = pl.ds(pl.multiple_of(xp * zx, zx), zx)
            for dz in ([0] if dx == 0 else []) + order(nz) + ([0] if dx else []):
                zp = lax.rem(z + dz, nz)
                src, dst = tz.at[p, c, zp, rows], tx.at[p, c, x, z]
                if dx == 0 and dz == 0:
                    near(src, dst, xr.at[p, c])
                else:
                    far(src, dst, xs.at[p, c], xr.at[p, c], xp * nz + zp, me_c)

    def x_stage(p, c):
        wait(xr.at[p, c], tx.at[p, c])
        rows = nz * zx
        for bit in range(nx.bit_length() - 1):
            level(tx.at[p, c], rows, nx, bit, xv1, xs1, xvn)

        @pl.when(z == 0)
        def _():
            root = tx[p, c, 0].reshape(rows, NB)
            inner = dot(wide(dot(wide(root), xv1[0])), xs1[0])
            tx[p, c, 0] = (root - dot_nt(wide(inner), xvn[0])).reshape(nz, zx, NB)

    def send_l(p, c):
        near(tx.at[p, c, x], back.at[p, c, :, x], lr.at[p, c])
        for dx in order(nx):
            xp = lax.rem(x + dx, nx)
            far(tx.at[p, c, xp], back.at[p, c, :, x], ls.at[p, c], lr.at[p, c], xp * nz + z, me_c)

    def out_rest(c):
        cols = pl.ds(pl.multiple_of(c * cw, cw), cw)
        near(work.at[pl.ds(NB, mr - NB), cols], out.at[pl.ds(NB, mr - NB), cols], osem)

    for p in range(npan):
        @pl.loop(0, nc)
        def _(c):
            if p:
                wait(lr.at[p - 1, c], back.at[p - 1, c])
            leaf_top(p, c)
            send_z(p, c)

        if p == 0:
            send_third(0, 0)
            send_third(1, 0)
            for q in range(1, npan):
                take_y(q)
                send_second(0, q)
                send_second(1, q)
        prep_pairs(0, p)

        @pl.loop(0, nc)
        def _(c):
            leaf_rest(p, c)
            if p == npan - 1:
                out_rest(c)

        @pl.loop(0, nc)
        def _(c):
            z_stage(p, c)
            send_x(p, c)

        prep_pairs(1, p)
        if p + 1 < npan:
            prep_leaf(p + 1)
            send_third(0, p + 1)
            send_third(1, p + 1)

            @pl.loop(0, nc)
            def _(c):
                next_part(p + 1, c)

        @pl.loop(0, nc)
        def _(c):
            x_stage(p, c)
            send_l(p, c)

    last = npan - 1

    @pl.loop(0, nc)
    def _(c):
        wait(lr.at[last, c], back.at[last, c])

        @pl.loop(0, tiles)
        def _(t):
            cols = column(c, t)
            held = back.at[last, c, pl.ds(t * (tw // zc), tw // zc)]
            work[:NB, cols] = held[...].reshape(tw, NB).T
        cols = pl.ds(pl.multiple_of(c * cw, cw), cw)
        near(work.at[pl.ds(0, NB), cols], out.at[pl.ds(0, NB), cols], osem)

    wait(osem, work)
    for p in range(npan):
        if ny > 1:
            wait(ys.at[p], yvec.at[p, pl.ds(0, ny - 1), 0])
            for k, buf in ((0, vsz), (1, vsx)):
                wait(hs.at[1, k, p], buf.at[p, pl.ds(0, ny - 1), 0])
        wait(ps.at[0, p], yvec.at[p, :, 0])
        for k, (buf, n) in enumerate(((vsz, nz), (vsx, nx))):
            wait(hs.at[0, k, p], buf.at[p, 0, 0, pl.ds(0, n - 1)])
            wait(ps.at[1 + k, p], buf.at[p, :, 0])

        @pl.loop(0, nc)
        def _(c):
            wait(zs.at[p, c], stay.at[p, c, pl.ds(0, nz - 1)])
            wait(xs.at[p, c], tx.at[p, c, pl.ds(0, nx - 1)])
            wait(xs.at[p, c], tx.at[p, c, 0, pl.ds(0, nz - 1)])
            wait(ls.at[p, c], tx.at[p, c, pl.ds(0, nx - 1)])


def local(nx, nc, window, leaf_vecs, leaf_t, node_vecs, node_t):
    mr, ncl = window.shape
    npan = leaf_t.shape[0]
    nz = lax.axis_size("row") // nx
    nq = lax.axis_size("col")
    ny = nq // CORES
    vr = NB // nq
    cw = ncl // nc
    zc = cw // nz
    zx = zc // nx
    any_space = pl.BlockSpec(memory_space=pl.ANY)
    dma = pltpu.SemaphoreType.DMA
    scratch = [
        pltpu.VMEM((mr, ncl), F32),
        pltpu.VMEM((npan, ny, CORES, mr // nq, NB), F32),
        pltpu.VMEM((npan, NB, NB), F32),
        pltpu.VMEM((npan, ny, CORES, nz, 2, vr, NB), F32),
        pltpu.VMEM((npan, ny, CORES, nx, 2, vr, NB), F32),
        pltpu.VMEM((npan, nc, nz, zc, NB), F32),
        pltpu.VMEM((npan, nc, nz, zc, NB), F32),
        pltpu.VMEM((npan, nc, nx, nz, zx, NB), F32),
        pltpu.VMEM((npan, nc, nz, nx, zx, NB), F32),
        pltpu.VMEM((NB, ncl), F32),
        pltpu.VMEM((3 * NB, ncl), BF16),
        pltpu.VMEM((npan, mr, 3 * NB), BF16),
        pltpu.VMEM((npan, 2 * NB, mr), BF16),
        pltpu.VMEM((npan, NB, 3 * NB), BF16),
    ]
    for n in (nz, nx):
        scratch += [
            pltpu.VMEM((n, 3 * NB, NB), BF16),
            pltpu.VMEM((n, 3 * NB, NB), BF16),
            pltpu.VMEM((n, NB, 3 * NB), BF16),
        ]
    scratch += [
        dma((5,)), dma((1,)), dma((npan,)), dma((npan,)), dma((3, npan)), dma((3, npan)),
        dma((2, 2, npan)), dma((2, 2, npan)),
        dma((npan, nc)), dma((npan, nc)), dma((npan, nc)), dma((npan, nc)), dma((npan, nc)), dma((npan, nc)),
        dma,
    ]
    return pl.pallas_call(
        functools.partial(kernel, (nx, nz, ny, nc, mr, ncl, npan)),
        out_shape=jax.ShapeDtypeStruct(window.shape, window.dtype),
        in_specs=[any_space] * 5,
        out_specs=any_space,
        scratch_shapes=scratch,
        compiler_params=pltpu.CompilerParams(
            collective_id=0, has_side_effects=True, vmem_limit_bytes=67_043_328
        ),
    )(
        window, leaf_vecs, leaf_t,
        node_vecs.reshape(npan, nq, vr, NB), node_t.reshape(npan, nq, vr, NB),
    )


def build(mesh, nx, nc):
    placed = (
        P("row", "col"),
        P(None, ("row", "col"), None),
        P(None, "row", None),
        P(None, "row", None),
        P(None, "row", None),
    )
    return jax.shard_map(
        functools.partial(local, nx, nc), mesh=mesh, in_specs=placed, out_specs=P("row", "col"), check_vma=False
    )


def solution(mesh):
    return build(mesh, NX, CHUNKS)
```
